512 devices in a mesh: rows: 64 (over z, y_hi, core), chan: 8 (over x, y_lo).
Axes of the slice: x: 4, y: 4 (y_hi: 2, y_lo: 2; y = y_hi * 2 + y_lo), z: 16, core: 2. Of those that a mesh axis runs over, the one named last changes fastest.
Arguments:
- features: bfloat16 [256, 128, 2048], P('rows', None, 'chan'), may hold values from 0 to 12, as said below
- low_features: bfloat16 [1024, 512, 256], P('rows', 'chan'), may hold values from -6 to 6
- w_one: bfloat16 [2048, 256], P('chan'), may hold values from -0.125 to 0.125
- w_rate: bfloat16 [3, 9, 2048, 256], P(None, None, 'chan', 'rows'), may hold values from -0.046875 to 0.046875
- w_pool: bfloat16 [2048, 256], P('chan'), may hold values from -0.125 to 0.125
- b_branch: float32 [5, 256], replicated, may hold values from -3 to 3
- w_proj: bfloat16 [1280, 256], replicated, may hold values from -0.15625 to 0.15625
- b_proj: float32 [256], replicated, may hold values from -3 to 3
- w_low: bfloat16 [256, 48], replicated, may hold values from -0.375 to 0.375
- b_low: float32 [48], replicated, may hold values from -3 to 3
- w_dec_up: bfloat16 [9, 256, 256], replicated, may hold values from -0.109375 to 0.109375
- w_dec_low: bfloat16 [9, 48, 256], replicated, may hold values from -0.109375 to 0.109375
- b_dec: float32 [256], replicated, may hold values from -3 to 3
Outputs:
- context: bfloat16 [256, 128, 256], P('rows', 'chan')
- decoded: bfloat16 [1024, 512, 256], P('rows', 'chan')
The draws below stay inside these ranges and needn't reach their ends.
Inputs may be any that keep to these rules, and one draw needn't show every extreme that they name: features are nonnegative.
All inputs are finite; a program needn't handle non-finite values.
Results may differ from the reference program's by a relative error of at most 0.019.
Values may be sent and summed in bfloat16 or wider, within the bound.
No kernel may reach another device: no remote copies, remote signals or barrier semaphores. Data moves between devices by JAX's collectives and lax.ppermute only.
A program may use at most 128 MiB of HBM per device.

```python
import math
import jax
import jax.numpy as jnp
from jax import lax

CIN = 2048
BR = 256
LOWC = 256
LOWP = 48
DEC = 256
RATE = 6
COLS = 128
GROUPS = 8
MAP_ROWS = 256
FINE_ROWS = 1024
FINE_COLS = 512


def draw_features(key, part):
    keys = jax.random.split(jax.random.fold_in(key, 11), 4)
    shape = (MAP_ROWS, COLS, CIN)
    position = jnp.arange(MAP_ROWS, dtype=jnp.float32) / MAP_ROWS
    base = jnp.abs(jax.random.normal(keys[0], shape, jnp.float32))
    rising = 3.0 ** position
    row_spread = jnp.exp(jax.random.uniform(keys[1], (MAP_ROWS,), jnp.float32, 0.0, math.log(10.0)))
    col_scale = jnp.exp(jax.random.uniform(keys[2], (COLS,), jnp.float32, 0.0, math.log(10.0)))
    chan_scale = jnp.exp(jax.random.uniform(keys[3], (CIN,), jnp.float32, -math.log(2.0), math.log(2.0)))
    row_scale = rising * row_spread
    values = base * row_scale[:, None, None] * col_scale[None, :, None] * chan_scale[None, None, :] / 24.0
    return jnp.minimum(values, 12.0).astype(jnp.bfloat16)


def shard_levels(rng, extent, pieces, smallest, high):
    level, own = 1.0, jax.random.fold_in(rng, 6)
    for axis_at, blocks in pieces:
        steps = jnp.exp(jax.random.uniform(jax.random.fold_in(own, axis_at), (blocks,), jnp.float32, smallest / len(pieces), high / len(pieces)))
        level = level * jnp.repeat(steps, extent[axis_at] // blocks).reshape([-1 if axis == axis_at else 1 for axis in range(len(extent))])
    return level


def bell_draw(stream_key, shape, spread, limit, cuts=(), kind=jnp.bfloat16):
    entries = jax.random.normal(stream_key, shape, jnp.float32) * spread
    if len(cuts) > 0:
        entries = shard_levels(stream_key, shape, cuts, -0.22, 0.18) * entries
    return jnp.clip(entries, min=-limit, max=limit).astype(kind)


def setup_inputs(seed: int = 0) -> dict:
    key_list = jax.random.split(jax.random.key(seed), 14)
    return {
        "features": draw_features(jax.random.fold_in(key_list[13], 71), 0),
        "low_features": bell_draw(key_list[1], (FINE_ROWS, FINE_COLS, LOWC), 1.0, 6.0, ((0, 64), (1, 8))),
        "w_one": bell_draw(key_list[2], (CIN, BR), CIN ** -0.5, 0.125, ((0, 8),)),
        "w_rate": bell_draw(key_list[3], (3, 9, CIN, BR), (9 * CIN) ** -0.5, 0.046875, ((2, 8), (3, 64))),
        "w_pool": bell_draw(key_list[4], (CIN, BR), CIN ** -0.5, 0.125, ((0, 8),)),
        "b_branch": bell_draw(key_list[5], (5, BR), 0.5, 3.0, (), jnp.float32),
        "w_proj": bell_draw(key_list[6], (5 * BR, BR), (5 * BR) ** -0.5, 0.15625),
        "b_proj": bell_draw(key_list[7], (BR,), 0.5, 3.0, (), jnp.float32),
        "w_low": bell_draw(key_list[8], (LOWC, LOWP), LOWC ** -0.5, 0.375),
        "b_low": bell_draw(key_list[9], (LOWP,), 0.5, 3.0, (), jnp.float32),
        "w_dec_up": bell_draw(key_list[10], (9, BR, DEC), (9 * (BR + LOWP)) ** -0.5, 0.109375),
        "w_dec_low": bell_draw(key_list[11], (9, LOWP, DEC), (9 * (BR + LOWP)) ** -0.5, 0.109375),
        "b_dec": bell_draw(key_list[12], (DEC,), 0.5, 3.0, (), jnp.float32),
    }


BLEND = (0.875, 0.625, 0.375, 0.125)


def moved(field, down, across):
    count_rows = field.shape[0]
    count_cols = field.shape[1]
    pad_rows = abs(down)
    pad_cols = abs(across)
    padded = jnp.pad(field, ((pad_rows, pad_rows), (pad_cols, pad_cols), (0, 0)))
    return padded[pad_rows + down:pad_rows + down + count_rows, pad_cols + across:pad_cols + across + count_cols]


def blend_axis(field, axis_pos):
    count_in = field.shape[axis_pos]
    lower_half = lax.slice_in_dim(field, 0, count_in - 1, axis=axis_pos)
    upper_half = lax.slice_in_dim(field, 1, count_in, axis=axis_pos)
    blended = jnp.stack([factor * lower_half + (1.0 - factor) * upper_half for factor in BLEND], axis=axis_pos + 1)
    target = list(lower_half.shape)
    target[axis_pos] = 4 * (count_in - 1)
    return blended.reshape(target)


def reference(features, low_features, w_one, w_rate, w_pool, b_branch, w_proj, b_proj, w_low, b_low, w_dec_up, w_dec_low, b_dec):
    map_rows, map_cols, channels = features.shape
    branch_width = w_one.shape[1]
    group_in = channels // GROUPS
    pixel_count = map_rows * map_cols

    def add_group(total, first_in):
        part_in = lax.dynamic_slice_in_dim(features, first_in, group_in, 2)
        one_weight = lax.dynamic_slice_in_dim(w_one, first_in, group_in, 0)
        rate_weight = lax.dynamic_slice_in_dim(w_rate, first_in, group_in, 2)
        outputs = [jnp.dot(part_in.reshape(pixel_count, group_in), one_weight, preferred_element_type=jnp.float32)]
        for rate_level in range(3):
            spacing = RATE * (rate_level + 1)
            accum = jnp.zeros((pixel_count, branch_width), jnp.float32)
            for tap_index in range(9):
                down = (tap_index // 3 - 1) * spacing
                across = (tap_index % 3 - 1) * spacing
                source = moved(part_in, down, across).reshape(pixel_count, group_in)
                accum = accum + jnp.dot(source, rate_weight[rate_level, tap_index], preferred_element_type=jnp.float32)
            outputs.append(accum)
        partial_value = jnp.concatenate(outputs, axis=1).astype(jnp.bfloat16)
        partial_value = lax.optimization_barrier(partial_value)
        return total + partial_value.astype(jnp.float32), None

    starts = jnp.arange(GROUPS, dtype=jnp.int32) * group_in
    zeros = jnp.zeros((pixel_count, 4 * branch_width), jnp.float32)
    branch_sum, unused = lax.scan(add_group, zeros, starts)
    branches = jax.nn.relu(branch_sum + b_branch[:4].reshape(-1)).astype(jnp.bfloat16)

    pooled = jnp.sum(features.astype(jnp.float32), axis=(0, 1)) / pixel_count
    pool_pre = jnp.dot(pooled, w_pool.astype(jnp.float32), precision=lax.Precision.HIGHEST)
    pool_branch = jax.nn.relu(pool_pre + b_branch[4]).astype(jnp.bfloat16)
    pool_term = jnp.dot(pool_branch[None, :], w_proj[4 * branch_width:], preferred_element_type=jnp.float32)[0]
    projected = jnp.dot(branches, w_proj[:4 * branch_width], preferred_element_type=jnp.float32)
    context = jax.nn.relu(projected + pool_term + b_proj).astype(jnp.bfloat16).reshape(map_rows, map_cols, branch_width)

    fine_rows, fine_cols = low_features.shape[0], low_features.shape[1]
    low_flat = low_features.reshape(fine_rows * fine_cols, low_features.shape[2])
    low_mapped = jax.nn.relu(jnp.dot(low_flat, w_low, preferred_element_type=jnp.float32) + b_low).astype(jnp.bfloat16)
    low_mapped = low_mapped.reshape(fine_rows, fine_cols, -1)

    edged = jnp.pad(context.astype(jnp.float32), ((1, 1), (1, 1), (0, 0)), mode="edge")
    upsampled = blend_axis(edged, 0)[2:4 * map_rows + 2]
    upsampled = blend_axis(upsampled, 1)[:, 2:4 * map_cols + 2].astype(jnp.bfloat16)

    up_pad = jnp.pad(upsampled, ((1, 1), (1, 1), (0, 0)))
    low_pad = jnp.pad(low_mapped, ((1, 1), (1, 1), (0, 0)))
    accum = jnp.zeros((fine_rows * fine_cols, w_dec_up.shape[2]), jnp.float32)
    for tap_index in range(9):
        row_step = tap_index // 3
        col_step = tap_index % 3
        up_slice = up_pad[row_step:row_step + fine_rows, col_step:col_step + fine_cols].reshape(fine_rows * fine_cols, -1)
        low_slice = low_pad[row_step:row_step + fine_rows, col_step:col_step + fine_cols].reshape(fine_rows * fine_cols, -1)
        accum = accum + jnp.dot(up_slice, w_dec_up[tap_index], preferred_element_type=jnp.float32)
        accum = accum + jnp.dot(low_slice, w_dec_low[tap_index], preferred_element_type=jnp.float32)
    decoded = jax.nn.relu(accum + b_dec).astype(jnp.bfloat16).reshape(fine_rows, fine_cols, -1)
    return context, decoded
```

```python
import functools

import jax
import jax.numpy as jnp
import numpy as np
from jax import lax
from jax.experimental import pallas as pl
from jax.experimental.pallas import tpu as pltpu
from jax.sharding import Mesh
from jax.sharding import PartitionSpec as P

RATE = 6
BLEND = (0.875, 0.625, 0.375, 0.125)
SPLIT = (("z", 16), ("yh", 2), ("core", 2), ("x", 4), ("yl", 2))
ROWS = ("z", "yh", "core")
CHAN = ("x", "yl")
BLOCK = ("x", "yl", "yh", "core")
BF = jnp.bfloat16
F32 = jnp.float32
STRIP = 4
EXT = 18
REACH = 19
UNIT = 120
PIECE = 112


def swap(axis):
    return [(0, 1), (1, 0)]


def shift_pairs(size, distance):
    return [(i, i + distance) for i in range(size) if 0 <= i + distance < size]


def halves(value):
    high = lax.reduce_precision(value, 8, 7)
    rest = value - high
    mid = lax.reduce_precision(rest, 8, 7)
    return high, mid, rest - mid


def dot_t(a, b):
    return lax.dot_general(a, b, (((1,), (1,)), ((), ())), preferred_element_type=F32)


def dot(a, b):
    return jnp.dot(a, b, preferred_element_type=F32)


def conv_kernel(
    place, eight, other, above, below, far, traded, packed, w_one, w_pool, out,
    x, rhs, wide, piece, sems,
):
    core = place[0]
    member = place[1]
    copies = []

    def fetch(source, first, count, target):
        index = len(copies)
        copy = pltpu.make_async_copy(
            source.at[pl.ds(first, count)], x.at[pl.ds(target, count)], sems.at[index]
        )
        copy.start()
        copies.append(copy)

    for half in range(2):
        mine = 8 * half + STRIP * core
        theirs = 8 * half + STRIP * (1 - core)
        fetch(eight, STRIP * half, STRIP, REACH + mine)
        fetch(other, STRIP * half, STRIP, REACH + theirs)
        fetch(above, STRIP * half, STRIP, REACH - 16 + mine)
        fetch(below, STRIP * half, STRIP, REACH + 16 + mine)
        fetch(traded, STRIP * half, STRIP, REACH - 16 + theirs)
        fetch(traded, 8 + STRIP * half, STRIP, REACH + 16 + theirs)
    fetch(far, 0, 3, 51 * (1 - core))
    fetch(traded, 16, 3, 51 * core)

    slot = (lax.broadcasted_iota(jnp.int32, (256, 256), 0) // 4) % 4
    for level in range(3):
        for index, (first, low, high) in enumerate(
            ((4 * level, 0, 2), (12 + 6 * level, 0, 2), (14 + 6 * level, 1, 3))
        ):
            rows = packed[:, 4 * first : 4 * first + 16, :].reshape(256, 256).astype(F32)
            keep = (slot >= low) & (slot <= high)
            rhs[3 * level + index] = jnp.where(keep, rows, 0.0).astype(BF)

    sums = jnp.sum(packed[:, 24:32, :].astype(F32), axis=0)
    pooled = (sums[4:5] + sums[5:6] + sums[6:7]) / float(256 * 128)
    pre = jnp.dot(
        jnp.broadcast_to(pooled, (8, 256)),
        w_pool[...].astype(F32),
        precision=lax.Precision.HIGHEST,
        preferred_element_type=F32,
    )[0:1]
    high = pre.astype(BF).astype(F32)
    mid = (pre - high).astype(BF).astype(F32)
    low = pre - high - mid
    piece[108:112, :] = jnp.concatenate([high, mid, low, jnp.zeros_like(low)], axis=0)

    wide[:, 0:8, :] = jnp.zeros((EXT, 8, 256), F32)
    wide[:, 136:144, :] = jnp.zeros((EXT, 8, 256), F32)

    for copy in copies:
        copy.wait()

    row_in = lax.broadcasted_iota(jnp.int32, (256, 256), 0)
    col_out = lax.broadcasted_iota(jnp.int32, (256, 256), 1)
    target = 4 * (row_in // 16) + row_in % 4
    lane_slot = (lax.broadcasted_iota(jnp.int32, (1, 128, 256), 2) // 4) % 4
    column = lax.broadcasted_iota(jnp.int32, (1, 128, 256), 1)
    picks = [(col_out == target + 64 * (level + 1)).astype(F32).astype(BF) for level in range(3)]
    own = (col_out == target) & ((row_in // 4) % 4 == member)
    pick_one = own.astype(F32).astype(BF)

    def chunk(step, carry):
        first = 6 * step
        centre = x[pl.ds(first + 18, 6)].reshape(768, 256)
        total = dot(dot(centre, w_one[...]).astype(BF), pick_one)
        for level in range(3):
            spacing = RATE * (level + 1)
            upper = x[pl.ds(first + 18 - spacing, 6)].reshape(768, 256)
            lower = x[pl.ds(first + 18 + spacing, 6)].reshape(768, 256)
            value = dot_t(centre, rhs[3 * level])
            value += dot_t(upper, rhs[3 * level + 1])
            value += dot_t(lower, rhs[3 * level + 2])
            value = value.reshape(6, 128, 256)
            from_left = ((lane_slot == 0) | (lane_slot == 3)) & (column >= spacing)
            from_right = (lane_slot == 2) & (column < 128 - spacing)
            moved = jnp.where(
                from_left,
                pltpu.roll(value, spacing, 1),
                jnp.where(
                    lane_slot == 1,
                    value,
                    jnp.where(from_right, pltpu.roll(value, 128 - spacing, 1), 0.0),
                ),
            ).reshape(768, 256)
            high = moved.astype(BF)
            low = (moved - high.astype(F32)).astype(BF)
            total += dot(high, picks[level]) + dot(low, picks[level])
        wide[pl.ds(first, 6), 8:136, :] = total.reshape(6, 128, 256)
        return carry

    lax.fori_loop(0, 3, chunk, 0)

    def send(part, carry):
        for tile in range(8):
            for line in range(6):
                piece[18 * line : 18 * line + 18, :] = wide[
                    STRIP * part + line, 16 * tile + 7 : 16 * tile + 25, :
                ]
            out[4 * tile + part] = piece[...].astype(BF)
        return carry

    lax.fori_loop(0, 4, send, 0)


def tail_kernel(
    received, w_proj, w_head, b_branch, b_pool, b_proj, blend, low, w_up, w_low, b_dec,
    context, decoded, cells, coarse, fine,
):
    pool = jnp.zeros((4, 256), F32)
    total = jnp.zeros((PIECE, 256), F32)
    for part in range(4):
        summed = received[part].astype(F32)
        for tile in range(1, 8):
            summed += received[4 * tile + part].astype(F32)
        pool += summed[108:112]
        branches = jnp.maximum(summed + b_branch[part : part + 1, :], 0.0).astype(BF)
        total += dot(branches, w_proj[part])
    pre = pool[0:1] + pool[1:2] + pool[2:3]
    pool_branch = jnp.maximum(pre + b_pool[...], 0.0)
    pool_term = dot(jnp.broadcast_to(pool_branch, (8, 256)).astype(BF), w_head[...])[0:1]
    value = jnp.maximum(total + pool_term + b_proj[...], 0.0)
    row = lax.broadcasted_iota(jnp.int32, (PIECE, 256), 0)
    value = jnp.where(row < 108, value, 0.0)
    cells[...] = value
    coarse[0:PIECE, :] = value.astype(BF)
    coarse[PIECE:128, :] = jnp.zeros((16, 256), BF)
    for line in range(4):
        context[line] = cells[18 * line + 19 : 18 * line + 35, :].astype(BF)
    for across in range(3):
        fine[across] = dot(blend[across], coarse[...]).astype(BF).reshape(EXT, 64, 256)
    for first in (0, 8):
        mixed = jnp.broadcast_to(b_dec[...], (512, 256))
        for down in range(3):
            mixed += dot(low[first + down : first + down + 8].reshape(512, 144), w_low[down])
            for across in range(3):
                up = fine[across, first + down : first + down + 8].reshape(512, 256)
                mixed += dot(up, w_up[3 * down + across])
        decoded[first : first + 8] = jnp.maximum(mixed, 0.0).astype(BF).reshape(8, 64, 256)


def blend_weights(count, fine_count, first, at_start, at_end):
    table = np.zeros((fine_count, count + 2), np.float32)
    for place in range(fine_count):
        index = place + first
        if (at_start and index < 2) or (at_end and index >= 4 * count + 2):
            continue
        pair, kind = divmod(index, 4)
        for cell, weight in ((pair, BLEND[kind]), (pair + 1, 1.0 - BLEND[kind])):
            cell = max(cell, 1) if at_start else cell
            cell = min(cell, count) if at_end else cell
            table[place, cell] += weight
    return table


def blend_matrix(row_index, row_count, tile_index, tile_count):
    cell = np.arange(128)
    valid = cell < 108

    def chosen(index, count, build):
        start, middle, end = build(True, False), build(False, False), build(False, True)
        value = jnp.where(index == 0, jnp.asarray(start), jnp.asarray(middle))
        return jnp.where(index == count - 1, jnp.asarray(end), value)

    def spread(table, source):
        return (table[:, np.where(valid, source, 0)] * valid).astype(np.float32)

    rows = chosen(
        row_index, row_count, lambda s, e: spread(blend_weights(4, EXT, 1, s, e), cell // 18)
    )
    blocks = []
    for across in range(3):
        cols = chosen(
            tile_index,
            tile_count,
            lambda s, e: spread(blend_weights(16, 64, 1 + across, s, e), cell % 18),
        )
        blocks.append((rows[:, None, :] * cols[None, :, :]).astype(BF).reshape(EXT * 64, 128))
    return jnp.stack(blocks)


def on_device(
    features,
    low_features,
    w_one,
    w_rate,
    w_pool,
    b_branch,
    w_proj,
    b_proj,
    w_low,
    b_low,
    w_dec_up,
    w_dec_low,
    b_dec,
):
    z_count = lax.axis_size("z")
    yh = lax.axis_index("yh")
    core = lax.axis_index("core")
    member = 2 * yh + core
    row_index = lax.axis_index(ROWS)
    row_count = lax.axis_size(ROWS)
    tile_index = lax.axis_index(CHAN)
    tile_count = lax.axis_size(CHAN)

    across_y = lax.ppermute(features, "yh", swap("yh"))
    across_y, w_rate, low_features = lax.optimization_barrier((across_y, w_rate, low_features))
    eight = jnp.where(
        yh == 0,
        jnp.concatenate([features, across_y], axis=0),
        jnp.concatenate([across_y, features], axis=0),
    )
    above = lax.ppermute(eight, "z", shift_pairs(z_count, 1))
    below = lax.ppermute(eight, "z", shift_pairs(z_count, -1))
    pairs = [(2 * i + 1, 2 * i + 5) for i in range(z_count - 2)]
    pairs += [(2 * i + 4, 2 * i) for i in range(z_count - 2)]
    far = lax.ppermute(jnp.where(core == 1, eight[5:8], eight[0:3]), ("z", "core"), pairs)
    other = lax.ppermute(eight, "core", swap("core"))

    low_flat = low_features.reshape(-1, low_features.shape[2])
    low_mapped = jax.nn.relu(jnp.dot(low_flat, w_low, preferred_element_type=F32) + b_low)
    low_mapped = low_mapped.astype(BF).reshape(16, 64, 48)
    left = lax.ppermute(low_mapped[:, 63:], CHAN, shift_pairs(tile_count, 1))
    right = lax.ppermute(low_mapped[:, :1], CHAN, shift_pairs(tile_count, -1))
    low_mapped = jnp.concatenate([left, low_mapped, right], axis=1)
    top = lax.ppermute(low_mapped[15:], ROWS, shift_pairs(row_count, 1))
    bottom = lax.ppermute(low_mapped[:1], ROWS, shift_pairs(row_count, -1))
    low_mapped = jnp.concatenate([top, low_mapped, bottom], axis=0)
    low_taps = jnp.concatenate([low_mapped[:, i : i + 64] for i in range(3)], axis=2)

    taps = jnp.transpose(w_rate, (0, 1, 3, 2))
    local_sum = jnp.sum(features, axis=(0, 1), dtype=F32)
    empty = jnp.zeros((1, 4, 256), BF)
    pool_rows = jnp.stack(halves(local_sum) + (jnp.zeros_like(local_sum),))[None].astype(BF)
    unit = []
    for level in range(3):
        unit += [taps[level, 3:6], pool_rows if level == 1 else empty]
    for level in range(3):
        unit += [taps[level, 0:3], taps[level, 7:9], taps[level, 6:7]]
    unit = jnp.concatenate(unit, axis=0).reshape(1, UNIT, 256)
    packed = lax.all_gather(unit, "z", axis=0, tiled=True)

    traded = lax.ppermute(jnp.concatenate([above, below, far], axis=0), "core", swap("core"))

    place = jnp.stack([core, member]).astype(jnp.int32)
    anywhere = pl.BlockSpec(memory_space=pl.ANY)
    on_chip = pl.BlockSpec(memory_space=pltpu.VMEM)
    pieces = pl.pallas_call(
        conv_kernel,
        name="branches",
        out_shape=jax.ShapeDtypeStruct((32, PIECE, 256), BF),
        in_specs=[pl.BlockSpec(memory_space=pltpu.SMEM)] + [anywhere] * 6 + [on_chip] * 3,
        out_specs=on_chip,
        scratch_shapes=[
            pltpu.VMEM((54, 128, 256), BF),
            pltpu.VMEM((9, 256, 256), BF),
            pltpu.VMEM((EXT, 144, 256), F32),
            pltpu.VMEM((PIECE, 256), F32),
            pltpu.SemaphoreType.DMA((14,)),
        ],
    )(place, eight, other, above, below, far, traded, packed, w_one, w_pool)
    received = lax.all_to_all(pieces, BLOCK, 0, 0, tiled=True)

    heads = w_proj[:1024].reshape(4, 16, 4, 4, 256).transpose(2, 0, 1, 3, 4).reshape(4, 256, 256)
    biases = b_branch[:4].reshape(4, 16, 4, 4).transpose(2, 0, 1, 3).reshape(4, 256)
    blend = blend_matrix(row_index, row_count, tile_index, tile_count)
    context, decoded = pl.pallas_call(
        tail_kernel,
        name="decoder",
        out_shape=(
            jax.ShapeDtypeStruct((4, 16, 256), BF),
            jax.ShapeDtypeStruct((16, 64, 256), BF),
        ),
        in_specs=[on_chip] * 11,
        out_specs=(on_chip, on_chip),
        scratch_shapes=[
            pltpu.VMEM((PIECE, 256), F32),
            pltpu.VMEM((128, 256), BF),
            pltpu.VMEM((3, EXT, 64, 256), BF),
        ],
    )(
        received,
        heads,
        w_proj[1024:],
        biases,
        b_branch[4:5],
        b_proj[None],
        blend,
        low_taps,
        w_dec_up,
        w_dec_low.reshape(3, 144, 256),
        b_dec[None],
    )
    return (context, decoded)


def solution(mesh):
    names = [name for name, size in SPLIT]
    sizes = [size for name, size in SPLIT]
    fine_mesh = Mesh(mesh.devices.reshape(sizes), names)
    in_specs = (
        P(ROWS, None, CHAN),
        P(ROWS, CHAN, None),
        P(CHAN, None),
        P(None, None, CHAN, ROWS),
        P(CHAN, None),
        P(),
        P(),
        P(),
        P(),
        P(),
        P(),
        P(),
        P(),
    )
    out_specs = (P(ROWS, CHAN, None), P(ROWS, CHAN, None))
    return jax.shard_map(
        on_device, mesh=fine_mesh, in_specs=in_specs, out_specs=out_specs, check_vma=False
    )
```

```python
import jax
import jax.numpy as jnp
import numpy as np
from jax import lax
from jax.experimental import pallas as pl
from jax.experimental.pallas import tpu as pltpu
from jax.sharding import Mesh
from jax.sharding import PartitionSpec as P

RATE = 6
BLEND = (0.875, 0.625, 0.375, 0.125)
SPLIT = (("z", 16), ("yh", 2), ("core", 2), ("x", 4), ("yl", 2))
ROWS = ("z", "yh", "core")
CHAN = ("x", "yl")
BLOCK = ("x", "yl", "yh", "core")
BF = jnp.bfloat16
F32 = jnp.float32
STRIP = 4
EXT = 18
REACH = 19
UNIT = 112
PIECE = 112


def swap():
    return [(0, 1), (1, 0)]


def shift_pairs(size, distance):
    return [(i, i + distance) for i in range(size) if 0 <= i + distance < size]


def halves(value):
    high = lax.reduce_precision(value, 8, 7)
    rest = value - high
    mid = lax.reduce_precision(rest, 8, 7)
    return high, mid, rest - mid


def dot_t(a, b):
    return lax.dot_general(a, b, (((1,), (1,)), ((), ())), preferred_element_type=F32)


def held(array):
    return pltpu.with_memory_space_constraint(array, pltpu.HBM)


def dot(a, b):
    return jnp.dot(a, b, preferred_element_type=F32)


def conv_kernel(
    place, mine, theirs, packed, w_one, w_pool, out,
    x, rhs, wide, piece, ready, sems, out_sems,
):
    core = place[0]
    member = place[1]
    copies = []

    def fetch(source, first, count, target):
        index = len(copies)
        copy = pltpu.make_async_copy(
            source.at[pl.ds(first, count)], x.at[pl.ds(target, count)], sems.at[index]
        )
        copy.start()
        copies.append(copy)

    for part, base in ((0, REACH), (1, REACH - 16), (2, REACH + 16)):
        for half in range(2):
            first = 8 * part + STRIP * half
            fetch(mine, first, STRIP, base + 8 * half + STRIP * core)
            fetch(theirs, first, STRIP, base + 8 * half + STRIP * (1 - core))
    fetch(mine, 24, 3, 51 * (1 - core))
    fetch(theirs, 24, 3, 51 * core)

    slot = (lax.broadcasted_iota(jnp.int32, (256, 256), 0) // 4) % 4
    for index in range(9):
        odd = index % 2
        first = 12 * index - 4 * odd
        rows = packed[:, first : first + 16, :].reshape(256, 256).astype(F32)
        keep = (slot >= odd) & (slot <= 2 + odd)
        rhs[index] = jnp.where(keep, rows, 0.0).astype(BF)

    sums = jnp.sum(packed[:, 104:112, :].astype(F32), axis=0)
    pooled = (sums[4:5] + sums[5:6] + sums[6:7]) / float(256 * 128)
    pre = jnp.dot(
        jnp.broadcast_to(pooled, (8, 256)),
        w_pool[...].astype(F32),
        precision=lax.Precision.HIGHEST,
        preferred_element_type=F32,
    )[0:1]
    high = pre.astype(BF).astype(F32)
    mid = (pre - high).astype(BF).astype(F32)
    low = pre - high - mid
    piece[108:112, :] = jnp.concatenate([high, mid, low, jnp.zeros_like(low)], axis=0)

    wide[:, 0:8, :] = jnp.zeros((EXT, 8, 256), F32)
    wide[:, 136:144, :] = jnp.zeros((EXT, 8, 256), F32)

    for copy in copies:
        copy.wait()

    row_in = lax.broadcasted_iota(jnp.int32, (256, 256), 0)
    col_out = lax.broadcasted_iota(jnp.int32, (256, 256), 1)
    target = 4 * (row_in // 16) + row_in % 4
    lane_slot = (lax.broadcasted_iota(jnp.int32, (1, 128, 256), 2) // 4) % 4
    column = lax.broadcasted_iota(jnp.int32, (1, 128, 256), 1)
    picks = [(col_out == target + 64 * (level + 1)).astype(F32).astype(BF) for level in range(3)]
    own = (col_out == target) & ((row_in // 4) % 4 == member)
    pick_one = own.astype(F32).astype(BF)

    def chunk(step, carry):
        first = 6 * step
        centre = x[pl.ds(first + 18, 6)].reshape(768, 256)
        total = dot(dot(centre, w_one[...]).astype(BF), pick_one)
        for level in range(3):
            spacing = RATE * (level + 1)
            upper = x[pl.ds(first + 18 - spacing, 6)].reshape(768, 256)
            lower = x[pl.ds(first + 18 + spacing, 6)].reshape(768, 256)
            value = dot_t(centre, rhs[3 * level])
            value += dot_t(upper, rhs[3 * level + 1])
            value += dot_t(lower, rhs[3 * level + 2])
            value = value.reshape(6, 128, 256)
            from_left = ((lane_slot == 0) | (lane_slot == 3)) & (column >= spacing)
            from_right = (lane_slot == 2) & (column < 128 - spacing)
            moved = jnp.where(
                from_left,
                pltpu.roll(value, spacing, 1),
                jnp.where(
                    lane_slot == 1,
                    value,
                    jnp.where(from_right, pltpu.roll(value, 128 - spacing, 1), 0.0),
                ),
            ).reshape(768, 256)
            total += dot(moved.astype(BF), picks[level])
        wide[pl.ds(first, 6), 8:136, :] = total.reshape(6, 128, 256)
        return carry

    lax.fori_loop(0, 3, chunk, 0)

    def put(slot, index):
        return pltpu.make_async_copy(ready.at[slot], out.at[index], out_sems.at[slot])

    def send(part, carry):
        for tile in range(8):
            slot = tile % 2
            for line in range(6):
                piece[18 * line : 18 * line + 18, :] = wide[
                    STRIP * part + line, 16 * tile + 7 : 16 * tile + 25, :
                ]
            if tile < 2:
                @pl.when(part > 0)
                def _():
                    put(slot, 4 * (tile + 6) + part - 1).wait()
            else:
                put(slot, 4 * (tile - 2) + part).wait()
            ready[slot] = piece[...].astype(BF)
            put(slot, 4 * tile + part).start()
        return carry

    lax.fori_loop(0, 4, send, 0)
    put(0, 4 * 6 + 3).wait()
    put(1, 4 * 7 + 3).wait()


def tail_kernel(
    received, heads, w_head, b_branch, b_pool, b_proj, blend, low, ups, lows, b_dec,
    context, decoded, cells, coarse, fine, w_proj, w_up, w_low, sems,
):
    copies = [
        pltpu.make_async_copy(source, target, sems.at[index])
        for index, (source, target) in enumerate(((heads, w_proj), (ups, w_up), (lows, w_low)))
    ]
    for copy in copies:
        copy.start()
    pool = jnp.zeros((4, 256), F32)
    total = jnp.zeros((PIECE, 256), F32)
    copies[0].wait()
    for part in range(4):
        summed = received[part].astype(F32)
        for tile in range(1, 8):
            summed += received[4 * tile + part].astype(F32)
        pool += summed[108:112]
        branches = jnp.maximum(summed + b_branch[part : part + 1, :], 0.0).astype(BF)
        total += dot(branches, w_proj[part])
    pre = pool[0:1] + pool[1:2] + pool[2:3]
    pool_branch = jnp.maximum(pre + b_pool[...], 0.0)
    pool_term = dot(jnp.broadcast_to(pool_branch, (8, 256)).astype(BF), w_head[...])[0:1]
    value = jnp.maximum(total + pool_term + b_proj[...], 0.0)
    row = lax.broadcasted_iota(jnp.int32, (PIECE, 256), 0)
    value = jnp.where(row < 108, value, 0.0)
    cells[...] = value
    coarse[0:PIECE, :] = value.astype(BF)
    coarse[PIECE:128, :] = jnp.zeros((16, 256), BF)
    for line in range(4):
        context[line] = cells[18 * line + 19 : 18 * line + 35, :].astype(BF)
    for across in range(3):
        fine[across] = dot(blend[across], coarse[...]).astype(BF).reshape(EXT, 64, 256)
    copies[1].wait()
    copies[2].wait()
    for first in (0, 8):
        mixed = jnp.broadcast_to(b_dec[...], (512, 256))
        for down in range(3):
            mixed += dot(low[first + down : first + down + 8].reshape(512, 144), w_low[down])
            for across in range(3):
                up = fine[across, first + down : first + down + 8].reshape(512, 256)
                mixed += dot(up, w_up[3 * down + across])
        decoded[first : first + 8] = jnp.maximum(mixed, 0.0).astype(BF).reshape(8, 64, 256)


def blend_weights(count, fine_count, first, at_start, at_end):
    table = np.zeros((fine_count, count + 2), np.float32)
    for place in range(fine_count):
        index = place + first
        if (at_start and index < 2) or (at_end and index >= 4 * count + 2):
            continue
        pair, kind = divmod(index, 4)
        for cell, weight in ((pair, BLEND[kind]), (pair + 1, 1.0 - BLEND[kind])):
            cell = max(cell, 1) if at_start else cell
            cell = min(cell, count) if at_end else cell
            table[place, cell] += weight
    return table


def blend_matrix(row_index, row_count, tile_index, tile_count):
    cell = np.arange(128)
    valid = cell < 108

    def chosen(index, count, build):
        start, middle, end = build(True, False), build(False, False), build(False, True)
        value = jnp.where(index == 0, jnp.asarray(start), jnp.asarray(middle))
        return jnp.where(index == count - 1, jnp.asarray(end), value)

    def spread(table, source):
        return (table[:, np.where(valid, source, 0)] * valid).astype(np.float32)

    rows = chosen(
        row_index, row_count, lambda s, e: spread(blend_weights(4, EXT, 1, s, e), cell // 18)
    )
    blocks = []
    for across in range(3):
        cols = chosen(
            tile_index,
            tile_count,
            lambda s, e: spread(blend_weights(16, 64, 1 + across, s, e), cell % 18),
        )
        blocks.append((rows[:, None, :] * cols[None, :, :]).astype(BF).reshape(EXT * 64, 128))
    return jnp.stack(blocks)


def tap_order():
    table = np.zeros((UNIT, 108), np.float32)
    taps = []
    for level in range(3):
        for part, first in enumerate((3, 0, 6)):
            first += 9 * level
            odd = (3 * level + part) % 2
            taps += [first + 1, first + 2, first] if odd else [first, first + 1, first + 2]
    for place, tap in enumerate(taps):
        for channel in range(4):
            table[4 * place + channel, 4 * tap + channel] = 1.0
    return table


def on_device(
    features,
    low_features,
    w_one,
    w_rate,
    w_pool,
    b_branch,
    w_proj,
    b_proj,
    w_low,
    b_low,
    w_dec_up,
    w_dec_low,
    b_dec,
):
    z_count = lax.axis_size("z")
    yh = lax.axis_index("yh")
    core = lax.axis_index("core")
    member = 2 * yh + core
    row_index = lax.axis_index(ROWS)
    row_count = lax.axis_size(ROWS)
    tile_index = lax.axis_index(CHAN)
    tile_count = lax.axis_size(CHAN)

    across_y = lax.ppermute(features, "yh", swap())

    low_flat = low_features.reshape(-1, low_features.shape[2])
    low_mapped = jax.nn.relu(jnp.dot(low_flat, w_low, preferred_element_type=F32) + b_low)
    low_mapped = low_mapped.astype(BF).reshape(16, 64, 48)
    taps = jnp.transpose(w_rate, (0, 1, 3, 2)).reshape(108, 256)
    unit = jnp.dot(jnp.asarray(tap_order(), BF), taps, preferred_element_type=F32)
    high, mid, rest = halves(jnp.sum(features, axis=(0, 1), dtype=F32)[None])
    line = lax.broadcasted_iota(jnp.int32, (UNIT, 256), 0)
    for index, value in enumerate((high, mid, rest)):
        unit = jnp.where(line == 108 + index, value, unit)
    unit = unit.astype(BF)[None]

    packed = lax.all_gather(unit, "z", axis=0, tiled=True)
    across_y, packed, low_mapped = lax.optimization_barrier((across_y, packed, low_mapped))
    eight = jnp.where(
        yh == 0,
        jnp.concatenate([features, across_y], axis=0),
        jnp.concatenate([across_y, features], axis=0),
    )
    ends = jnp.where(
        core == 1,
        jnp.where(yh == 0, across_y[1:4], features[1:4]),
        jnp.where(yh == 0, features[0:3], across_y[0:3]),
    )
    above = lax.ppermute(eight, "z", shift_pairs(z_count, 1))
    below = lax.ppermute(eight, "z", shift_pairs(z_count, -1))
    pairs = [(2 * i + 1, 2 * i + 5) for i in range(z_count - 2)]
    pairs += [(2 * i + 4, 2 * i) for i in range(z_count - 2)]
    far = lax.ppermute(ends, ("z", "core"), pairs)
    left = lax.ppermute(low_mapped[:, 63:], CHAN, shift_pairs(tile_count, 1))
    right = lax.ppermute(low_mapped[:, :1], CHAN, shift_pairs(tile_count, -1))
    low_mapped = jnp.concatenate([left, low_mapped, right], axis=1)
    above, below, far, low_mapped = lax.optimization_barrier((above, below, far, low_mapped))
    joint = jnp.concatenate([eight, above, below, far], axis=0)
    traded = lax.ppermute(joint, "core", swap())

    place = jnp.stack([core, member]).astype(jnp.int32)
    on_chip = pl.BlockSpec(memory_space=pltpu.VMEM)
    anywhere = pl.BlockSpec(memory_space=pl.ANY)
    in_hbm = pl.BlockSpec(memory_space=pltpu.HBM)
    pieces = pl.pallas_call(
        conv_kernel,
        name="branches",
        out_shape=jax.ShapeDtypeStruct((32, PIECE, 256), BF),
        in_specs=[pl.BlockSpec(memory_space=pltpu.SMEM)] + [anywhere] * 2 + [on_chip] * 3,
        out_specs=in_hbm,
        scratch_shapes=[
            pltpu.VMEM((54, 128, 256), BF),
            pltpu.VMEM((9, 256, 256), BF),
            pltpu.VMEM((EXT, 144, 256), F32),
            pltpu.VMEM((PIECE, 256), F32),
            pltpu.VMEM((2, PIECE, 256), BF),
            pltpu.SemaphoreType.DMA((14,)),
            pltpu.SemaphoreType.DMA((2,)),
        ],
        compiler_params=pltpu.CompilerParams(vmem_limit_bytes=28 << 20),
    )(place, joint, traded, packed, w_one, w_pool)
    pieces = held(pieces)
    received = lax.all_to_all(pieces, BLOCK, 0, 0, tiled=True)
    top = lax.ppermute(low_mapped[15:], ROWS, shift_pairs(row_count, 1))
    bottom = lax.ppermute(low_mapped[:1], ROWS, shift_pairs(row_count, -1))
    low_mapped = jnp.concatenate([top, low_mapped, bottom], axis=0)
    low_taps = jnp.concatenate([low_mapped[:, i : i + 64] for i in range(3)], axis=2)

    heads = w_proj[:1024].reshape(4, 16, 4, 4, 256).transpose(2, 0, 1, 3, 4).reshape(4, 256, 256)
    biases = b_branch[:4].reshape(4, 16, 4, 4).transpose(2, 0, 1, 3).reshape(4, 256)
    blend = blend_matrix(row_index, row_count, tile_index, tile_count)
    context, decoded = pl.pallas_call(
        tail_kernel,
        name="decoder",
        out_shape=(
            jax.ShapeDtypeStruct((4, 16, 256), BF),
            jax.ShapeDtypeStruct((16, 64, 256), BF),
        ),
        in_specs=[on_chip, in_hbm] + [on_chip] * 6 + [in_hbm] * 2 + [on_chip],
        out_specs=(on_chip, on_chip),
        scratch_shapes=[
            pltpu.VMEM((PIECE, 256), F32),
            pltpu.VMEM((128, 256), BF),
            pltpu.VMEM((3, EXT, 64, 256), BF),
            pltpu.VMEM((4, 256, 256), BF),
            pltpu.VMEM((9, 256, 256), BF),
            pltpu.VMEM((3, 144, 256), BF),
            pltpu.SemaphoreType.DMA((3,)),
        ],
        compiler_params=pltpu.CompilerParams(vmem_limit_bytes=20 << 20),
    )(
        received,
        held(heads),
        w_proj[1024:],
        biases,
        b_branch[4:5],
        b_proj[None],
        blend,
        low_taps,
        held(w_dec_up),
        held(w_dec_low.reshape(3, 144, 256)),
        b_dec[None],
    )
    return (context, decoded)


def solution(mesh):
    names = [name for name, size in SPLIT]
    sizes = [size for name, size in SPLIT]
    fine_mesh = Mesh(mesh.devices.reshape(sizes), names)
    in_specs = (
        P(ROWS, None, CHAN),
        P(ROWS, CHAN, None),
        P(CHAN, None),
        P(None, None, CHAN, ROWS),
        P(CHAN, None),
        P(),
        P(),
        P(),
        P(),
        P(),
        P(),
        P(),
        P(),
    )
    out_specs = (P(ROWS, CHAN, None), P(ROWS, CHAN, None))

    return jax.shard_map(
        on_device, mesh=fine_mesh, in_specs=in_specs, out_specs=out_specs, check_vma=False
    )
```

```python
import jax
import jax.numpy as jnp
import numpy as np
from jax import lax
from jax.experimental import pallas as pl
from jax.experimental.pallas import tpu as pltpu
from jax.sharding import Mesh
from jax.sharding import PartitionSpec as P

RATE = 6
BLEND = (0.875, 0.625, 0.375, 0.125)
SPLIT = (("z", 16), ("yh", 2), ("core", 2), ("x", 4), ("yl", 2))
ROWS = ("z", "yh", "core")
CHAN = ("x", "yl")
BLOCK = ("x", "yl", "yh", "core")
BF = jnp.bfloat16
F32 = jnp.float32
STRIP = 4
EXT = 18
REACH = 19
UNIT = 112
PIECE = 112


def swap():
    return [(0, 1), (1, 0)]


def shift_pairs(size, distance):
    return [(i, i + distance) for i in range(size) if 0 <= i + distance < size]


def halves(value):
    high = lax.reduce_precision(value, 8, 7)
    rest = value - high
    mid = lax.reduce_precision(rest, 8, 7)
    return high, mid, rest - mid


def dot_t(a, b):
    return lax.dot_general(a, b, (((1,), (1,)), ((), ())), preferred_element_type=F32)


def held(array):
    return pltpu.with_memory_space_constraint(array, pltpu.HBM)


def dot(a, b):
    return jnp.dot(a, b, preferred_element_type=F32)


def conv_kernel(
    place, mine, theirs, packed, w_one, w_pool, out,
    x, rhs, wide, piece, ready, sems, out_sems,
):
    core = place[0]
    member = place[1]
    copies = []

    def fetch(source, first, count, target):
        index = len(copies)
        copy = pltpu.make_async_copy(
            source.at[pl.ds(first, count)], x.at[pl.ds(target, count)], sems.at[index]
        )
        copy.start()
        copies.append(copy)

    for part, base in ((0, REACH), (1, REACH - 16), (2, REACH + 16)):
        for half in range(2):
            first = 8 * part + STRIP * half
            fetch(mine, first, STRIP, base + 8 * half + STRIP * core)
            fetch(theirs, first, STRIP, base + 8 * half + STRIP * (1 - core))
    fetch(mine, 24, 3, 51 * (1 - core))
    fetch(theirs, 24, 3, 51 * core)

    slot = (lax.broadcasted_iota(jnp.int32, (256, 256), 0) // 4) % 4
    for index in range(9):
        odd = index % 2
        first = 12 * index - 4 * odd
        rows = packed[:, first : first + 16, :].reshape(256, 256).astype(F32)
        keep = (slot >= odd) & (slot <= 2 + odd)
        rhs[index] = jnp.where(keep, rows, 0.0).astype(BF)

    sums = jnp.sum(packed[:, 104:112, :].astype(F32), axis=0)
    pooled = (sums[4:5] + sums[5:6] + sums[6:7]) / float(256 * 128)
    pre = jnp.dot(
        jnp.broadcast_to(pooled, (8, 256)),
        w_pool[...].astype(F32),
        precision=lax.Precision.HIGHEST,
        preferred_element_type=F32,
    )[0:1]
    high = pre.astype(BF).astype(F32)
    mid = (pre - high).astype(BF).astype(F32)
    low = pre - high - mid
    piece[108:112, :] = jnp.concatenate([high, mid, low, jnp.zeros_like(low)], axis=0)

    wide[:, 0:8, :] = jnp.zeros((EXT, 8, 256), F32)
    wide[:, 136:144, :] = jnp.zeros((EXT, 8, 256), F32)

    for copy in copies:
        copy.wait()

    row_in = lax.broadcasted_iota(jnp.int32, (256, 256), 0)
    col_out = lax.broadcasted_iota(jnp.int32, (256, 256), 1)
    target = 4 * (row_in // 16) + row_in % 4
    lane_slot = (lax.broadcasted_iota(jnp.int32, (1, 128, 256), 2) // 4) % 4
    column = lax.broadcasted_iota(jnp.int32, (1, 128, 256), 1)
    picks = [(col_out == target + 64 * (level + 1)).astype(F32).astype(BF) for level in range(3)]
    own = (col_out == target) & ((row_in // 4) % 4 == member)
    pick_one = own.astype(F32).astype(BF)

    def chunk(step, carry):
        first = 9 * step
        centre = x[pl.ds(first + 18, 9)].reshape(1152, 256)
        total = dot(dot(centre, w_one[...]).astype(BF), pick_one)
        for level in range(3):
            spacing = RATE * (level + 1)
            upper = x[pl.ds(first + 18 - spacing, 9)].reshape(1152, 256)
            lower = x[pl.ds(first + 18 + spacing, 9)].reshape(1152, 256)
            value = dot_t(centre, rhs[3 * level])
            value += dot_t(upper, rhs[3 * level + 1])
            value += dot_t(lower, rhs[3 * level + 2])
            value = value.reshape(9, 128, 256)
            from_left = ((lane_slot == 0) | (lane_slot == 3)) & (column >= spacing)
            from_right = (lane_slot == 2) & (column < 128 - spacing)
            moved = jnp.where(
                from_left,
                pltpu.roll(value, spacing, 1),
                jnp.where(
                    lane_slot == 1,
                    value,
                    jnp.where(from_right, pltpu.roll(value, 128 - spacing, 1), 0.0),
                ),
            ).reshape(1152, 256)
            total += dot(moved.astype(BF), picks[level])
        wide[pl.ds(first, 9), 8:136, :] = total.reshape(9, 128, 256)
        return carry

    lax.fori_loop(0, 2, chunk, 0)

    def put(index):
        return pltpu.make_async_copy(ready.at[index], out.at[index], out_sems.at[index])

    def send(part, carry):
        for tile in range(8):
            for line in range(6):
                piece[18 * line : 18 * line + 18, :] = wide[
                    STRIP * part + line, 16 * tile + 7 : 16 * tile + 25, :
                ]
            ready[4 * tile + part] = piece[...].astype(BF)
            put(4 * tile + part).start()
        return carry

    lax.fori_loop(0, 4, send, 0)

    def settle(index, carry):
        put(index).wait()
        return carry

    lax.fori_loop(0, 32, settle, 0)


def tail_kernel(
    received, heads, w_head, b_branch, b_pool, b_proj, blend, low, ups, lows, b_dec,
    context, decoded, cells, coarse, fine, w_proj, w_up, w_low, sems,
):
    copies = [
        pltpu.make_async_copy(source, target, sems.at[index])
        for index, (source, target) in enumerate(((heads, w_proj), (ups, w_up), (lows, w_low)))
    ]
    for copy in copies:
        copy.start()
    pool = jnp.zeros((4, 256), F32)
    total = jnp.zeros((PIECE, 256), F32)
    copies[0].wait()
    for part in range(4):
        summed = received[part].astype(F32)
        for tile in range(1, 8):
            summed += received[4 * tile + part].astype(F32)
        pool += summed[108:112]
        branches = jnp.maximum(summed + b_branch[part : part + 1, :], 0.0).astype(BF)
        total += dot(branches, w_proj[part])
    pre = pool[0:1] + pool[1:2] + pool[2:3]
    pool_branch = jnp.maximum(pre + b_pool[...], 0.0)
    pool_term = dot(jnp.broadcast_to(pool_branch, (8, 256)).astype(BF), w_head[...])[0:1]
    value = jnp.maximum(total + pool_term + b_proj[...], 0.0)
    row = lax.broadcasted_iota(jnp.int32, (PIECE, 256), 0)
    value = jnp.where(row < 108, value, 0.0)
    cells[...] = value
    coarse[0:PIECE, :] = value.astype(BF)
    coarse[PIECE:128, :] = jnp.zeros((16, 256), BF)
    for line in range(4):
        context[line] = cells[18 * line + 19 : 18 * line + 35, :].astype(BF)
    for across in range(3):
        fine[across] = dot(blend[across], coarse[...]).astype(BF).reshape(EXT, 64, 256)
    copies[1].wait()
    copies[2].wait()
    for first in (0, 8):
        mixed = jnp.broadcast_to(b_dec[...], (512, 256))
        for down in range(3):
            mixed += dot(low[first + down : first + down + 8].reshape(512, 144), w_low[down])
            for across in range(3):
                up = fine[across, first + down : first + down + 8].reshape(512, 256)
                mixed += dot(up, w_up[3 * down + across])
        decoded[first : first + 8] = jnp.maximum(mixed, 0.0).astype(BF).reshape(8, 64, 256)


def blend_weights(count, fine_count, first, at_start, at_end):
    table = np.zeros((fine_count, count + 2), np.float32)
    for place in range(fine_count):
        index = place + first
        if (at_start and index < 2) or (at_end and index >= 4 * count + 2):
            continue
        pair, kind = divmod(index, 4)
        for cell, weight in ((pair, BLEND[kind]), (pair + 1, 1.0 - BLEND[kind])):
            cell = max(cell, 1) if at_start else cell
            cell = min(cell, count) if at_end else cell
            table[place, cell] += weight
    return table


def blend_matrix(row_index, row_count, tile_index, tile_count):
    cell = np.arange(128)
    valid = cell < 108

    def chosen(index, count, build):
        start, middle, end = build(True, False), build(False, False), build(False, True)
        value = jnp.where(index == 0, jnp.asarray(start), jnp.asarray(middle))
        return jnp.where(index == count - 1, jnp.asarray(end), value)

    def spread(table, source):
        return (table[:, np.where(valid, source, 0)] * valid).astype(np.float32)

    rows = chosen(
        row_index, row_count, lambda s, e: spread(blend_weights(4, EXT, 1, s, e), cell // 18)
    )
    blocks = []
    for across in range(3):
        cols = chosen(
            tile_index,
            tile_count,
            lambda s, e: spread(blend_weights(16, 64, 1 + across, s, e), cell % 18),
        )
        blocks.append((rows[:, None, :] * cols[None, :, :]).astype(BF).reshape(EXT * 64, 128))
    return jnp.stack(blocks)


def tap_order():
    table = np.zeros((UNIT, 108), np.float32)
    taps = []
    for level in range(3):
        for part, first in enumerate((3, 0, 6)):
            first += 9 * level
            odd = (3 * level + part) % 2
            taps += [first + 1, first + 2, first] if odd else [first, first + 1, first + 2]
    for place, tap in enumerate(taps):
        for channel in range(4):
            table[4 * place + channel, 4 * tap + channel] = 1.0
    return table


def on_device(
    features,
    low_features,
    w_one,
    w_rate,
    w_pool,
    b_branch,
    w_proj,
    b_proj,
    w_low,
    b_low,
    w_dec_up,
    w_dec_low,
    b_dec,
):
    z_count = lax.axis_size("z")
    yh = lax.axis_index("yh")
    core = lax.axis_index("core")
    member = 2 * yh + core
    row_index = lax.axis_index(ROWS)
    row_count = lax.axis_size(ROWS)
    tile_index = lax.axis_index(CHAN)
    tile_count = lax.axis_size(CHAN)

    across_y = lax.ppermute(features, "yh", swap())

    taps = jnp.transpose(w_rate, (0, 1, 3, 2)).reshape(108, 256)
    unit = jnp.dot(jnp.asarray(tap_order(), BF), taps, preferred_element_type=F32)
    high, mid, rest = halves(jnp.sum(features, axis=(0, 1), dtype=F32)[None])
    line = lax.broadcasted_iota(jnp.int32, (UNIT, 256), 0)
    for index, value in enumerate((high, mid, rest)):
        unit = jnp.where(line == 108 + index, value, unit)
    unit = unit.astype(BF)[None]

    packed = lax.all_gather(unit, "z", axis=0, tiled=True)
    across_y, packed, low_features = lax.optimization_barrier((across_y, packed, low_features))
    low_flat = low_features.reshape(-1, low_features.shape[2])
    low_mapped = jax.nn.relu(jnp.dot(low_flat, w_low, preferred_element_type=F32) + b_low)
    low_mapped = low_mapped.astype(BF).reshape(16, 64, 48)
    eight = jnp.where(
        yh == 0,
        jnp.concatenate([features, across_y], axis=0),
        jnp.concatenate([across_y, features], axis=0),
    )
    ends = jnp.where(
        core == 1,
        jnp.where(yh == 0, across_y[1:4], features[1:4]),
        jnp.where(yh == 0, features[0:3], across_y[0:3]),
    )
    above = lax.ppermute(eight, "z", shift_pairs(z_count, 1))
    below = lax.ppermute(eight, "z", shift_pairs(z_count, -1))
    pairs = [(2 * i + 1, 2 * i + 5) for i in range(z_count - 2)]
    pairs += [(2 * i + 4, 2 * i) for i in range(z_count - 2)]
    far = lax.ppermute(ends, ("z", "core"), pairs)
    left = lax.ppermute(low_mapped[:, 63:], CHAN, shift_pairs(tile_count, 1))
    right = lax.ppermute(low_mapped[:, :1], CHAN, shift_pairs(tile_count, -1))
    low_mapped = jnp.concatenate([left, low_mapped, right], axis=1)
    above, below, far, low_mapped = lax.optimization_barrier((above, below, far, low_mapped))
    joint = jnp.concatenate([eight, above, below, far], axis=0)
    traded = lax.ppermute(joint, "core", swap())

    place = jnp.stack([core, member]).astype(jnp.int32)
    on_chip = pl.BlockSpec(memory_space=pltpu.VMEM)
    anywhere = pl.BlockSpec(memory_space=pl.ANY)
    in_hbm = pl.BlockSpec(memory_space=pltpu.HBM)
    pieces = pl.pallas_call(
        conv_kernel,
        name="branches",
        out_shape=jax.ShapeDtypeStruct((32, PIECE, 256), BF),
        in_specs=[pl.BlockSpec(memory_space=pltpu.SMEM)] + [anywhere] * 2 + [on_chip] * 3,
        out_specs=in_hbm,
        scratch_shapes=[
            pltpu.VMEM((54, 128, 256), BF),
            pltpu.VMEM((9, 256, 256), BF),
            pltpu.VMEM((EXT, 144, 256), F32),
            pltpu.VMEM((PIECE, 256), F32),
            pltpu.VMEM((32, PIECE, 256), BF),
            pltpu.SemaphoreType.DMA((14,)),
            pltpu.SemaphoreType.DMA((32,)),
        ],
        compiler_params=pltpu.CompilerParams(vmem_limit_bytes=28 << 20),
    )(place, joint, traded, packed, w_one, w_pool)
    pieces = held(pieces)
    received = lax.all_to_all(pieces, BLOCK, 0, 0, tiled=True)
    top = lax.ppermute(low_mapped[15:], ROWS, shift_pairs(row_count, 1))
    bottom = lax.ppermute(low_mapped[:1], ROWS, shift_pairs(row_count, -1))
    low_mapped = jnp.concatenate([top, low_mapped, bottom], axis=0)
    low_taps = jnp.concatenate([low_mapped[:, i : i + 64] for i in range(3)], axis=2)

    heads = w_proj[:1024].reshape(4, 16, 4, 4, 256).transpose(2, 0, 1, 3, 4).reshape(4, 256, 256)
    biases = b_branch[:4].reshape(4, 16, 4, 4).transpose(2, 0, 1, 3).reshape(4, 256)
    blend = blend_matrix(row_index, row_count, tile_index, tile_count)
    context, decoded = pl.pallas_call(
        tail_kernel,
        name="decoder",
        out_shape=(
            jax.ShapeDtypeStruct((4, 16, 256), BF),
            jax.ShapeDtypeStruct((16, 64, 256), BF),
        ),
        in_specs=[on_chip, in_hbm] + [on_chip] * 6 + [in_hbm] * 2 + [on_chip],
        out_specs=(on_chip, on_chip),
        scratch_shapes=[
            pltpu.VMEM((PIECE, 256), F32),
            pltpu.VMEM((128, 256), BF),
            pltpu.VMEM((3, EXT, 64, 256), BF),
            pltpu.VMEM((4, 256, 256), BF),
            pltpu.VMEM((9, 256, 256), BF),
            pltpu.VMEM((3, 144, 256), BF),
            pltpu.SemaphoreType.DMA((3,)),
        ],
        compiler_params=pltpu.CompilerParams(vmem_limit_bytes=20 << 20),
    )(
        received,
        held(heads),
        w_proj[1024:],
        biases,
        b_branch[4:5],
        b_proj[None],
        blend,
        low_taps,
        held(w_dec_up),
        held(w_dec_low.reshape(3, 144, 256)),
        b_dec[None],
    )
    return (context, decoded)


def solution(mesh):
    names = [name for name, size in SPLIT]
    sizes = [size for name, size in SPLIT]
    fine_mesh = Mesh(mesh.devices.reshape(sizes), names)
    in_specs = (
        P(ROWS, None, CHAN),
        P(ROWS, CHAN, None),
        P(CHAN, None),
        P(None, None, CHAN, ROWS),
        P(CHAN, None),
        P(),
        P(),
        P(),
        P(),
        P(),
        P(),
        P(),
        P(),
    )
    out_specs = (P(ROWS, CHAN, None), P(ROWS, CHAN, None))

    return jax.shard_map(
        on_device, mesh=fine_mesh, in_specs=in_specs, out_specs=out_specs, check_vma=False
    )
```

```python
import jax
import jax.numpy as jnp
import numpy as np
from jax import lax
from jax.experimental import pallas as pl
from jax.experimental.pallas import tpu as pltpu
from jax.sharding import Mesh
from jax.sharding import PartitionSpec as P

RATE = 6
BLEND = (0.875, 0.625, 0.375, 0.125)
SPLIT = (("z", 16), ("yh", 2), ("core", 2), ("x", 4), ("yl", 2))
ROWS = ("z", "yh", "core")
CHAN = ("x", "yl")
BLOCK = ("x", "yl", "yh", "core")
BF = jnp.bfloat16
F32 = jnp.float32
STRIP = 4
EXT = 18
REACH = 19
UNIT = 112
PIECE = 112


def swap():
    return [(0, 1), (1, 0)]


def shift_pairs(size, distance):
    return [(i, i + distance) for i in range(size) if 0 <= i + distance < size]


def halves(value):
    high = lax.reduce_precision(value, 8, 7)
    rest = value - high
    mid = lax.reduce_precision(rest, 8, 7)
    return high, mid, rest - mid


def dot_t(a, b):
    return lax.dot_general(a, b, (((1,), (1,)), ((), ())), preferred_element_type=F32)


def held(array):
    return pltpu.with_memory_space_constraint(array, pltpu.HBM)


def dot(a, b):
    return jnp.dot(a, b, preferred_element_type=F32)


def conv_kernel(
    place, mine, theirs, packed, w_one, w_pool, out,
    x, rhs, wide, piece, ready, sems, out_sems,
):
    core = place[0]
    member = place[1]
    copies = []

    def fetch(source, first, count, target):
        index = len(copies)
        copy = pltpu.make_async_copy(
            source.at[pl.ds(first, count)], x.at[pl.ds(target, count)], sems.at[index]
        )
        copy.start()
        copies.append(copy)

    for part, base in ((0, REACH), (1, REACH - 16), (2, REACH + 16)):
        for half in range(2):
            first = 8 * part + STRIP * half
            fetch(mine, first, STRIP, base + 8 * half + STRIP * core)
            fetch(theirs, first, STRIP, base + 8 * half + STRIP * (1 - core))
    fetch(mine, 24, 3, 51 * (1 - core))
    fetch(theirs, 24, 3, 51 * core)

    slot = (lax.broadcasted_iota(jnp.int32, (256, 256), 0) // 4) % 4
    for index in range(9):
        odd = index % 2
        first = 12 * index - 4 * odd
        rows = packed[:, first : first + 16, :].reshape(256, 256).astype(F32)
        keep = (slot >= odd) & (slot <= 2 + odd)
        rhs[index] = jnp.where(keep, rows, 0.0).astype(BF)

    sums = jnp.sum(packed[:, 104:112, :].astype(F32), axis=0)
    pooled = (sums[4:5] + sums[5:6] + sums[6:7]) / float(256 * 128)
    pre = jnp.dot(
        jnp.broadcast_to(pooled, (8, 256)),
        w_pool[...].astype(F32),
        precision=lax.Precision.HIGHEST,
        preferred_element_type=F32,
    )[0:1]
    high = pre.astype(BF).astype(F32)
    mid = (pre - high).astype(BF).astype(F32)
    low = pre - high - mid
    piece[108:112, :] = jnp.concatenate([high, mid, low, jnp.zeros_like(low)], axis=0)

    wide[:, 0:8, :] = jnp.zeros((EXT, 8, 256), F32)
    wide[:, 136:144, :] = jnp.zeros((EXT, 8, 256), F32)

    for copy in copies:
        copy.wait()

    row_in = lax.broadcasted_iota(jnp.int32, (256, 256), 0)
    col_out = lax.broadcasted_iota(jnp.int32, (256, 256), 1)
    target = 4 * (row_in // 16) + row_in % 4
    lane_slot = (lax.broadcasted_iota(jnp.int32, (1, 128, 256), 2) // 4) % 4
    column = lax.broadcasted_iota(jnp.int32, (1, 128, 256), 1)
    picks = [(col_out == target + 64 * (level + 1)).astype(F32).astype(BF) for level in range(3)]
    own = (col_out == target) & ((row_in // 4) % 4 == member)
    pick_one = own.astype(F32).astype(BF)

    def chunk(step, carry):
        first = 9 * step
        centre = x[pl.ds(first + 18, 9)].reshape(1152, 256)
        total = dot(dot(centre, w_one[...]).astype(BF), pick_one)
        for level in range(3):
            spacing = RATE * (level + 1)
            upper = x[pl.ds(first + 18 - spacing, 9)].reshape(1152, 256)
            lower = x[pl.ds(first + 18 + spacing, 9)].reshape(1152, 256)
            value = dot_t(centre, rhs[3 * level])
            value += dot_t(upper, rhs[3 * level + 1])
            value += dot_t(lower, rhs[3 * level + 2])
            value = value.reshape(9, 128, 256)
            from_left = ((lane_slot == 0) | (lane_slot == 3)) & (column >= spacing)
            from_right = (lane_slot == 2) & (column < 128 - spacing)
            moved = jnp.where(
                from_left,
                pltpu.roll(value, spacing, 1),
                jnp.where(
                    lane_slot == 1,
                    value,
                    jnp.where(from_right, pltpu.roll(value, 128 - spacing, 1), 0.0),
                ),
            ).reshape(1152, 256)
            total += dot(moved.astype(BF), picks[level])
        wide[pl.ds(first, 9), 8:136, :] = total.reshape(9, 128, 256)
        return carry

    lax.fori_loop(0, 2, chunk, 0)

    def put(index):
        return pltpu.make_async_copy(ready.at[index], out.at[index], out_sems.at[index])

    def send(part, carry):
        for tile in range(8):
            for line in range(6):
                piece[18 * line : 18 * line + 18, :] = wide[
                    STRIP * part + line, 16 * tile + 7 : 16 * tile + 25, :
                ]
            ready[4 * tile + part] = piece[...].astype(BF)
            put(4 * tile + part).start()
        return carry

    lax.fori_loop(0, 4, send, 0)

    def settle(index, carry):
        put(index).wait()
        return carry

    lax.fori_loop(0, 32, settle, 0)


def low_kernel(low_features, w_low, b_low, out):
    value = dot(low_features[...], w_low[...]) + b_low[...]
    out[...] = jnp.maximum(value, 0.0).astype(BF)


def tail_kernel(
    received, heads, w_head, b_branch, b_pool, b_proj, blend, low, ups, lows, b_dec,
    context, decoded, cells, coarse, fine, w_proj, w_up, w_low, sems,
):
    copies = [
        pltpu.make_async_copy(source, target, sems.at[index])
        for index, (source, target) in enumerate(((heads, w_proj), (ups, w_up), (lows, w_low)))
    ]
    for copy in copies:
        copy.start()
    pool = jnp.zeros((4, 256), F32)
    total = jnp.zeros((PIECE, 256), F32)
    copies[0].wait()
    for part in range(4):
        summed = received[part].astype(F32)
        for tile in range(1, 8):
            summed += received[4 * tile + part].astype(F32)
        pool += summed[108:112]
        branches = jnp.maximum(summed + b_branch[part : part + 1, :], 0.0).astype(BF)
        total += dot(branches, w_proj[part])
    pre = pool[0:1] + pool[1:2] + pool[2:3]
    pool_branch = jnp.maximum(pre + b_pool[...], 0.0)
    pool_term = dot(jnp.broadcast_to(pool_branch, (8, 256)).astype(BF), w_head[...])[0:1]
    value = jnp.maximum(total + pool_term + b_proj[...], 0.0)
    row = lax.broadcasted_iota(jnp.int32, (PIECE, 256), 0)
    value = jnp.where(row < 108, value, 0.0)
    cells[...] = value
    coarse[0:PIECE, :] = value.astype(BF)
    coarse[PIECE:128, :] = jnp.zeros((16, 256), BF)
    for line in range(4):
        context[line] = cells[18 * line + 19 : 18 * line + 35, :].astype(BF)
    for across in range(3):
        fine[across] = dot(blend[across], coarse[...]).astype(BF).reshape(EXT, 64, 256)
    copies[1].wait()
    copies[2].wait()
    for first in (0, 8):
        mixed = jnp.broadcast_to(b_dec[...], (512, 256))
        for down in range(3):
            mixed += dot(low[first + down : first + down + 8].reshape(512, 144), w_low[down])
            for across in range(3):
                up = fine[across, first + down : first + down + 8].reshape(512, 256)
                mixed += dot(up, w_up[3 * down + across])
        decoded[first : first + 8] = jnp.maximum(mixed, 0.0).astype(BF).reshape(8, 64, 256)


def blend_weights(count, fine_count, first, at_start, at_end):
    table = np.zeros((fine_count, count + 2), np.float32)
    for place in range(fine_count):
        index = place + first
        if (at_start and index < 2) or (at_end and index >= 4 * count + 2):
            continue
        pair, kind = divmod(index, 4)
        for cell, weight in ((pair, BLEND[kind]), (pair + 1, 1.0 - BLEND[kind])):
            cell = max(cell, 1) if at_start else cell
            cell = min(cell, count) if at_end else cell
            table[place, cell] += weight
    return table


def blend_matrix(row_index, row_count, tile_index, tile_count):
    cell = np.arange(128)
    valid = cell < 108

    def chosen(index, count, build):
        start, middle, end = build(True, False), build(False, False), build(False, True)
        value = jnp.where(index == 0, jnp.asarray(start), jnp.asarray(middle))
        return jnp.where(index == count - 1, jnp.asarray(end), value)

    def spread(table, source):
        return (table[:, np.where(valid, source, 0)] * valid).astype(np.float32)

    rows = chosen(
        row_index, row_count, lambda s, e: spread(blend_weights(4, EXT, 1, s, e), cell // 18)
    )
    blocks = []
    for across in range(3):
        cols = chosen(
            tile_index,
            tile_count,
            lambda s, e: spread(blend_weights(16, 64, 1 + across, s, e), cell % 18),
        )
        blocks.append((rows[:, None, :] * cols[None, :, :]).astype(BF).reshape(EXT * 64, 128))
    return jnp.stack(blocks)


def tap_order():
    table = np.zeros((UNIT, 108), np.float32)
    taps = []
    for level in range(3):
        for part, first in enumerate((3, 0, 6)):
            first += 9 * level
            odd = (3 * level + part) % 2
            taps += [first + 1, first + 2, first] if odd else [first, first + 1, first + 2]
    for place, tap in enumerate(taps):
        for channel in range(4):
            table[4 * place + channel, 4 * tap + channel] = 1.0
    return table


def on_device(
    features,
    low_features,
    w_one,
    w_rate,
    w_pool,
    b_branch,
    w_proj,
    b_proj,
    w_low,
    b_low,
    w_dec_up,
    w_dec_low,
    b_dec,
):
    z_count = lax.axis_size("z")
    yh = lax.axis_index("yh")
    core = lax.axis_index("core")
    member = 2 * yh + core
    row_index = lax.axis_index(ROWS)
    row_count = lax.axis_size(ROWS)
    tile_index = lax.axis_index(CHAN)
    tile_count = lax.axis_size(CHAN)

    across_y = lax.ppermute(features, "yh", swap())

    taps = jnp.transpose(w_rate, (0, 1, 3, 2)).reshape(108, 256)
    unit = jnp.dot(jnp.asarray(tap_order(), BF), taps, preferred_element_type=F32)
    high, mid, rest = halves(jnp.sum(features, axis=(0, 1), dtype=F32)[None])
    line = lax.broadcasted_iota(jnp.int32, (UNIT, 256), 0)
    for index, value in enumerate((high, mid, rest)):
        unit = jnp.where(line == 108 + index, value, unit)
    unit = unit.astype(BF)[None]

    packed = lax.all_gather(unit, "z", axis=0, tiled=True)
    across_y, packed, low_features = lax.optimization_barrier((across_y, packed, low_features))
    low_flat = low_features.reshape(-1, low_features.shape[2])
    low_mapped = pl.pallas_call(
        low_kernel,
        name="low",
        out_shape=jax.ShapeDtypeStruct((1024, 48), BF),
        in_specs=[pl.BlockSpec(memory_space=pltpu.VMEM)] * 3,
        out_specs=pl.BlockSpec(memory_space=pltpu.VMEM),
        compiler_params=pltpu.CompilerParams(vmem_limit_bytes=4 << 20),
    )(low_flat, w_low, b_low[None]).reshape(16, 64, 48)
    eight = jnp.where(
        yh == 0,
        jnp.concatenate([features, across_y], axis=0),
        jnp.concatenate([across_y, features], axis=0),
    )
    ends = jnp.where(
        core == 1,
        jnp.where(yh == 0, across_y[1:4], features[1:4]),
        jnp.where(yh == 0, features[0:3], across_y[0:3]),
    )
    above = lax.ppermute(eight, "z", shift_pairs(z_count, 1))
    below = lax.ppermute(eight, "z", shift_pairs(z_count, -1))
    pairs = [(2 * i + 1, 2 * i + 5) for i in range(z_count - 2)]
    pairs += [(2 * i + 4, 2 * i) for i in range(z_count - 2)]
    far = lax.ppermute(ends, ("z", "core"), pairs)
    left = lax.ppermute(low_mapped[:, 63:], CHAN, shift_pairs(tile_count, 1))
    right = lax.ppermute(low_mapped[:, :1], CHAN, shift_pairs(tile_count, -1))
    low_mapped = jnp.concatenate([left, low_mapped, right], axis=1)
    above, below, far, low_mapped = lax.optimization_barrier((above, below, far, low_mapped))
    joint = jnp.concatenate([eight, above, below, far], axis=0)
    traded = lax.ppermute(joint, "core", swap())

    place = jnp.stack([core, member]).astype(jnp.int32)
    on_chip = pl.BlockSpec(memory_space=pltpu.VMEM)
    anywhere = pl.BlockSpec(memory_space=pl.ANY)
    in_hbm = pl.BlockSpec(memory_space=pltpu.HBM)
    pieces = pl.pallas_call(
        conv_kernel,
        name="branches",
        out_shape=jax.ShapeDtypeStruct((32, PIECE, 256), BF),
        in_specs=[pl.BlockSpec(memory_space=pltpu.SMEM)] + [anywhere] * 2 + [on_chip] * 3,
        out_specs=in_hbm,
        scratch_shapes=[
            pltpu.VMEM((54, 128, 256), BF),
            pltpu.VMEM((9, 256, 256), BF),
            pltpu.VMEM((EXT, 144, 256), F32),
            pltpu.VMEM((PIECE, 256), F32),
            pltpu.VMEM((32, PIECE, 256), BF),
            pltpu.SemaphoreType.DMA((14,)),
            pltpu.SemaphoreType.DMA((32,)),
        ],
        compiler_params=pltpu.CompilerParams(vmem_limit_bytes=52 << 20),
    )(place, joint, traded, packed, w_one, w_pool)
    pieces = held(pieces)
    received = lax.all_to_all(pieces, BLOCK, 0, 0, tiled=True)
    top = lax.ppermute(low_mapped[15:], ROWS, shift_pairs(row_count, 1))
    bottom = lax.ppermute(low_mapped[:1], ROWS, shift_pairs(row_count, -1))
    low_mapped = jnp.concatenate([top, low_mapped, bottom], axis=0)
    low_taps = jnp.concatenate([low_mapped[:, i : i + 64] for i in range(3)], axis=2)

    heads = w_proj[:1024].reshape(4, 16, 4, 4, 256).transpose(2, 0, 1, 3, 4).reshape(4, 256, 256)
    biases = b_branch[:4].reshape(4, 16, 4, 4).transpose(2, 0, 1, 3).reshape(4, 256)
    blend = blend_matrix(row_index, row_count, tile_index, tile_count)
    context, decoded = pl.pallas_call(
        tail_kernel,
        name="decoder",
        out_shape=(
            jax.ShapeDtypeStruct((4, 16, 256), BF),
            jax.ShapeDtypeStruct((16, 64, 256), BF),
        ),
        in_specs=[on_chip, in_hbm] + [on_chip] * 6 + [in_hbm] * 2 + [on_chip],
        out_specs=(on_chip, on_chip),
        scratch_shapes=[
            pltpu.VMEM((PIECE, 256), F32),
            pltpu.VMEM((128, 256), BF),
            pltpu.VMEM((3, EXT, 64, 256), BF),
            pltpu.VMEM((4, 256, 256), BF),
            pltpu.VMEM((9, 256, 256), BF),
            pltpu.VMEM((3, 144, 256), BF),
            pltpu.SemaphoreType.DMA((3,)),
        ],
        compiler_params=pltpu.CompilerParams(vmem_limit_bytes=20 << 20),
    )(
        pltpu.with_memory_space_constraint(received, pltpu.VMEM),
        held(heads),
        w_proj[1024:],
        biases,
        b_branch[4:5],
        b_proj[None],
        blend,
        low_taps,
        held(w_dec_up),
        held(w_dec_low.reshape(3, 144, 256)),
        b_dec[None],
    )
    return (context, decoded)


def solution(mesh):
    names = [name for name, size in SPLIT]
    sizes = [size for name, size in SPLIT]
    fine_mesh = Mesh(mesh.devices.reshape(sizes), names)
    in_specs = (
        P(ROWS, None, CHAN),
        P(ROWS, CHAN, None),
        P(CHAN, None),
        P(None, None, CHAN, ROWS),
        P(CHAN, None),
        P(),
        P(),
        P(),
        P(),
        P(),
        P(),
        P(),
        P(),
    )
    out_specs = (P(ROWS, CHAN, None), P(ROWS, CHAN, None))

    return jax.shard_map(
        on_device, mesh=fine_mesh, in_specs=in_specs, out_specs=out_specs, check_vma=False
    )
```

```python
import jax
import jax.numpy as jnp
import numpy as np
from jax import lax
from jax.experimental import pallas as pl
from jax.experimental.pallas import tpu as pltpu
from jax.sharding import Mesh
from jax.sharding import PartitionSpec as P

RATE = 6
BLEND = (0.875, 0.625, 0.375, 0.125)
SPLIT = (("z", 16), ("yh", 2), ("core", 2), ("x", 4), ("yl", 2))
ROWS = ("z", "yh", "core")
CHAN = ("x", "yl")
BLOCK = ("x", "yl", "yh", "core")
BF = jnp.bfloat16
F32 = jnp.float32
STRIP = 4
EXT = 18
REACH = 19
UNIT = 112
PIECE = 112


def swap():
    return [(0, 1), (1, 0)]


def shift_pairs(size, distance):
    return [(i, i + distance) for i in range(size) if 0 <= i + distance < size]


def halves(value):
    high = lax.reduce_precision(value, 8, 7)
    rest = value - high
    mid = lax.reduce_precision(rest, 8, 7)
    return high, mid, rest - mid


def dot_t(a, b):
    return lax.dot_general(a, b, (((1,), (1,)), ((), ())), preferred_element_type=F32)


def held(array):
    return pltpu.with_memory_space_constraint(array, pltpu.HBM)


def dot(a, b):
    return jnp.dot(a, b, preferred_element_type=F32)


def conv_kernel(
    place, mine, theirs, packed, w_one, w_pool, out,
    x, rhs, wide, piece, ready, sems, out_sems,
):
    core = place[0]
    member = place[1]
    copies = []

    def fetch(source, first, count, target):
        index = len(copies)
        copy = pltpu.make_async_copy(
            source.at[pl.ds(first, count)], x.at[pl.ds(target, count)], sems.at[index]
        )
        copy.start()
        copies.append(copy)

    for part, base in ((0, REACH), (1, REACH - 16), (2, REACH + 16)):
        for half in range(2):
            first = 8 * part + STRIP * half
            fetch(mine, first, STRIP, base + 8 * half + STRIP * core)
            fetch(theirs, first, STRIP, base + 8 * half + STRIP * (1 - core))
    fetch(mine, 24, 3, 51 * (1 - core))
    fetch(theirs, 24, 3, 51 * core)

    slot = (lax.broadcasted_iota(jnp.int32, (256, 256), 0) // 4) % 4
    for index in range(9):
        odd = index % 2
        first = 12 * index - 4 * odd
        rows = packed[:, first : first + 16, :].reshape(256, 256).astype(F32)
        keep = (slot >= odd) & (slot <= 2 + odd)
        rhs[index] = jnp.where(keep, rows, 0.0).astype(BF)

    sums = jnp.sum(packed[:, 104:112, :].astype(F32), axis=0)
    pooled = (sums[4:5] + sums[5:6] + sums[6:7]) / float(256 * 128)
    pre = jnp.dot(
        jnp.broadcast_to(pooled, (8, 256)),
        w_pool[...].astype(F32),
        precision=lax.Precision.HIGHEST,
        preferred_element_type=F32,
    )[0:1]
    high = pre.astype(BF).astype(F32)
    mid = (pre - high).astype(BF).astype(F32)
    low = pre - high - mid
    piece[108:112, :] = jnp.concatenate([high, mid, low, jnp.zeros_like(low)], axis=0)

    wide[:, 0:8, :] = jnp.zeros((EXT, 8, 256), F32)
    wide[:, 136:144, :] = jnp.zeros((EXT, 8, 256), F32)

    for copy in copies:
        copy.wait()

    row_in = lax.broadcasted_iota(jnp.int32, (256, 256), 0)
    col_out = lax.broadcasted_iota(jnp.int32, (256, 256), 1)
    target = 4 * (row_in // 16) + row_in % 4
    lane_slot = (lax.broadcasted_iota(jnp.int32, (1, 128, 256), 2) // 4) % 4
    column = lax.broadcasted_iota(jnp.int32, (1, 128, 256), 1)
    picks = [(col_out == target + 64 * (level + 1)).astype(F32).astype(BF) for level in range(3)]
    own = (col_out == target) & ((row_in // 4) % 4 == member)
    pick_one = own.astype(F32).astype(BF)

    def chunk(step, carry):
        first = 9 * step
        centre = x[pl.ds(first + 18, 9)].reshape(1152, 256)
        total = dot(dot(centre, w_one[...]).astype(BF), pick_one)
        for level in range(3):
            spacing = RATE * (level + 1)
            upper = x[pl.ds(first + 18 - spacing, 9)].reshape(1152, 256)
            lower = x[pl.ds(first + 18 + spacing, 9)].reshape(1152, 256)
            value = dot_t(centre, rhs[3 * level])
            value += dot_t(upper, rhs[3 * level + 1])
            value += dot_t(lower, rhs[3 * level + 2])
            value = value.reshape(9, 128, 256)
            from_left = ((lane_slot == 0) | (lane_slot == 3)) & (column >= spacing)
            from_right = (lane_slot == 2) & (column < 128 - spacing)
            moved = jnp.where(
                from_left,
                pltpu.roll(value, spacing, 1),
                jnp.where(
                    lane_slot == 1,
                    value,
                    jnp.where(from_right, pltpu.roll(value, 128 - spacing, 1), 0.0),
                ),
            ).reshape(1152, 256)
            total += dot(moved.astype(BF), picks[level])
        wide[pl.ds(first, 9), 8:136, :] = total.reshape(9, 128, 256)
        return carry

    lax.fori_loop(0, 2, chunk, 0)

    def put(index):
        return pltpu.make_async_copy(ready.at[index], out.at[index], out_sems.at[index])

    def send(part, carry):
        for tile in range(8):
            for line in range(6):
                piece[18 * line : 18 * line + 18, :] = wide[
                    STRIP * part + line, 16 * tile + 7 : 16 * tile + 25, :
                ]
            ready[4 * tile + part] = piece[...].astype(BF)
            put(4 * tile + part).start()
        return carry

    lax.fori_loop(0, 4, send, 0)

    def settle(index, carry):
        put(index).wait()
        return carry

    lax.fori_loop(0, 32, settle, 0)


def low_kernel(low_features, w_low, b_low, out):
    value = dot_t(low_features[...], w_low[...]) + b_low[...]
    out[...] = jnp.maximum(value, 0.0).astype(BF)


def tail_kernel(
    received, heads, w_head, b_branch, b_pool, b_proj, blend, low, ups, lows, b_dec,
    context, decoded, cells, coarse, mixes, w_proj, w_up, w_low, sems,
):
    copies = [
        pltpu.make_async_copy(source, target, sems.at[index])
        for index, (source, target) in enumerate(((heads, w_proj), (ups, w_up), (lows, w_low)))
    ]
    for copy in copies:
        copy.start()
    pool = jnp.zeros((4, 256), F32)
    total = jnp.zeros((PIECE, 256), F32)
    copies[0].wait()
    for part in range(4):
        summed = received[part].astype(F32)
        for tile in range(1, 8):
            summed += received[4 * tile + part].astype(F32)
        pool += summed[108:112]
        branches = jnp.maximum(summed + b_branch[part : part + 1, :], 0.0).astype(BF)
        total += dot(branches, w_proj[part])
    pre = pool[0:1] + pool[1:2] + pool[2:3]
    pool_branch = jnp.maximum(pre + b_pool[...], 0.0)
    pool_term = dot(jnp.broadcast_to(pool_branch, (8, 256)).astype(BF), w_head[...])[0:1]
    value = jnp.maximum(total + pool_term + b_proj[...], 0.0)
    row = lax.broadcasted_iota(jnp.int32, (PIECE, 256), 0)
    value = jnp.where(row < 108, value, 0.0)
    cells[...] = value
    coarse[0:PIECE, :] = value.astype(BF)
    coarse[PIECE:128, :] = jnp.zeros((16, 256), BF)
    for line in range(4):
        context[line] = cells[18 * line + 19 : 18 * line + 35, :].astype(BF)
    copies[1].wait()
    for tap in range(9):
        mixes[128 * tap : 128 * tap + 128, :] = dot(coarse[...], w_up[tap]).astype(BF)
    copies[2].wait()

    def cells_of(tap, first):
        down, across = divmod(tap, 3)
        return blend[across, 64 * (first + down) : 64 * (first + down) + 512, :]

    for first in (0, 8):
        mixed = jnp.broadcast_to(b_dec[...], (512, 256))
        for down in range(3):
            mixed += dot(low[first + down : first + down + 8].reshape(512, 144), w_low[down])
        for tap in (0, 2, 4, 6):
            pair = jnp.concatenate([cells_of(tap, first), cells_of(tap + 1, first)], axis=1)
            mixed += dot(pair, mixes[128 * tap : 128 * tap + 256, :])
        mixed += dot(cells_of(8, first), mixes[1024:1152, :])
        decoded[first : first + 8] = jnp.maximum(mixed, 0.0).astype(BF).reshape(8, 64, 256)


def blend_weights(count, fine_count, first, at_start, at_end):
    table = np.zeros((fine_count, count + 2), np.float32)
    for place in range(fine_count):
        index = place + first
        if (at_start and index < 2) or (at_end and index >= 4 * count + 2):
            continue
        pair, kind = divmod(index, 4)
        for cell, weight in ((pair, BLEND[kind]), (pair + 1, 1.0 - BLEND[kind])):
            cell = max(cell, 1) if at_start else cell
            cell = min(cell, count) if at_end else cell
            table[place, cell] += weight
    return table


def blend_matrix(row_index, row_count, tile_index, tile_count):
    cell = np.arange(128)
    valid = cell < 108

    def chosen(index, count, build):
        start, middle, end = build(True, False), build(False, False), build(False, True)
        value = jnp.where(index == 0, jnp.asarray(start), jnp.asarray(middle))
        return jnp.where(index == count - 1, jnp.asarray(end), value)

    def spread(table, source):
        return (table[:, np.where(valid, source, 0)] * valid).astype(np.float32)

    rows = chosen(
        row_index, row_count, lambda s, e: spread(blend_weights(4, EXT, 1, s, e), cell // 18)
    )
    blocks = []
    for across in range(3):
        cols = chosen(
            tile_index,
            tile_count,
            lambda s, e: spread(blend_weights(16, 64, 1 + across, s, e), cell % 18),
        )
        blocks.append((rows[:, None, :] * cols[None, :, :]).astype(BF).reshape(EXT * 64, 128))
    return jnp.stack(blocks)


def tap_order():
    table = np.zeros((UNIT, 108), np.float32)
    taps = []
    for level in range(3):
        for part, first in enumerate((3, 0, 6)):
            first += 9 * level
            odd = (3 * level + part) % 2
            taps += [first + 1, first + 2, first] if odd else [first, first + 1, first + 2]
    for place, tap in enumerate(taps):
        for channel in range(4):
            table[4 * place + channel, 4 * tap + channel] = 1.0
    return table


def on_device(
    features,
    low_features,
    w_one,
    w_rate,
    w_pool,
    b_branch,
    w_proj,
    b_proj,
    w_low,
    b_low,
    w_dec_up,
    w_dec_low,
    b_dec,
):
    z_count = lax.axis_size("z")
    yh = lax.axis_index("yh")
    core = lax.axis_index("core")
    member = 2 * yh + core
    row_index = lax.axis_index(ROWS)
    row_count = lax.axis_size(ROWS)
    tile_index = lax.axis_index(CHAN)
    tile_count = lax.axis_size(CHAN)

    across_y = lax.ppermute(features, "yh", swap())

    taps = jnp.transpose(w_rate, (0, 1, 3, 2)).reshape(108, 256)
    unit = jnp.dot(jnp.asarray(tap_order(), BF), taps, preferred_element_type=F32)
    high, mid, rest = halves(jnp.sum(features, axis=(0, 1), dtype=F32)[None])
    line = lax.broadcasted_iota(jnp.int32, (UNIT, 256), 0)
    for index, value in enumerate((high, mid, rest)):
        unit = jnp.where(line == 108 + index, value, unit)
    unit = unit.astype(BF)[None]

    packed = lax.all_gather(unit, "z", axis=0, tiled=True)
    across_y, packed, low_features = lax.optimization_barrier((across_y, packed, low_features))
    low_flat = low_features.reshape(-1, low_features.shape[2])
    low_mapped = pl.pallas_call(
        low_kernel,
        name="low",
        out_shape=jax.ShapeDtypeStruct((1024, 48), BF),
        in_specs=[pl.BlockSpec(memory_space=pltpu.VMEM)] * 3,
        out_specs=pl.BlockSpec(memory_space=pltpu.VMEM),
        compiler_params=pltpu.CompilerParams(vmem_limit_bytes=4 << 20),
    )(low_flat, w_low.T, b_low[None]).reshape(16, 64, 48)
    eight = jnp.where(
        yh == 0,
        jnp.concatenate([features, across_y], axis=0),
        jnp.concatenate([across_y, features], axis=0),
    )
    ends = jnp.where(
        core == 1,
        jnp.where(yh == 0, across_y[1:4], features[1:4]),
        jnp.where(yh == 0, features[0:3], across_y[0:3]),
    )
    above = lax.ppermute(eight, "z", shift_pairs(z_count, 1))
    below = lax.ppermute(eight, "z", shift_pairs(z_count, -1))
    pairs = [(2 * i + 1, 2 * i + 5) for i in range(z_count - 2)]
    pairs += [(2 * i + 4, 2 * i) for i in range(z_count - 2)]
    far = lax.ppermute(ends, ("z", "core"), pairs)
    left = lax.ppermute(low_mapped[:, 63:], CHAN, shift_pairs(tile_count, 1))
    right = lax.ppermute(low_mapped[:, :1], CHAN, shift_pairs(tile_count, -1))
    low_mapped = jnp.concatenate([left, low_mapped, right], axis=1)
    above, below, far, low_mapped = lax.optimization_barrier((above, below, far, low_mapped))
    joint = jnp.concatenate([eight, above, below, far], axis=0)
    traded = lax.ppermute(joint, "core", swap())

    place = jnp.stack([core, member]).astype(jnp.int32)
    on_chip = pl.BlockSpec(memory_space=pltpu.VMEM)
    anywhere = pl.BlockSpec(memory_space=pl.ANY)
    in_hbm = pl.BlockSpec(memory_space=pltpu.HBM)
    pieces = pl.pallas_call(
        conv_kernel,
        name="branches",
        out_shape=jax.ShapeDtypeStruct((32, PIECE, 256), BF),
        in_specs=[pl.BlockSpec(memory_space=pltpu.SMEM)] + [anywhere] * 2 + [on_chip] * 3,
        out_specs=in_hbm,
        scratch_shapes=[
            pltpu.VMEM((54, 128, 256), BF),
            pltpu.VMEM((9, 256, 256), BF),
            pltpu.VMEM((EXT, 144, 256), F32),
            pltpu.VMEM((PIECE, 256), F32),
            pltpu.VMEM((32, PIECE, 256), BF),
            pltpu.SemaphoreType.DMA((14,)),
            pltpu.SemaphoreType.DMA((32,)),
        ],
        compiler_params=pltpu.CompilerParams(vmem_limit_bytes=52 << 20),
    )(place, joint, traded, packed, w_one, w_pool)
    pieces = held(pieces)
    received = lax.all_to_all(pieces, BLOCK, 0, 0, tiled=True)
    top = lax.ppermute(low_mapped[15:], ROWS, shift_pairs(row_count, 1))
    bottom = lax.ppermute(low_mapped[:1], ROWS, shift_pairs(row_count, -1))
    low_mapped = jnp.concatenate([top, low_mapped, bottom], axis=0)
    low_taps = jnp.concatenate([low_mapped[:, i : i + 64] for i in range(3)], axis=2)

    heads = w_proj[:1024].reshape(4, 16, 4, 4, 256).transpose(2, 0, 1, 3, 4).reshape(4, 256, 256)
    biases = b_branch[:4].reshape(4, 16, 4, 4).transpose(2, 0, 1, 3).reshape(4, 256)
    blend = blend_matrix(row_index, row_count, tile_index, tile_count)
    context, decoded = pl.pallas_call(
        tail_kernel,
        name="decoder",
        out_shape=(
            jax.ShapeDtypeStruct((4, 16, 256), BF),
            jax.ShapeDtypeStruct((16, 64, 256), BF),
        ),
        in_specs=[on_chip, in_hbm] + [on_chip] * 6 + [in_hbm] * 2 + [on_chip],
        out_specs=(on_chip, on_chip),
        scratch_shapes=[
            pltpu.VMEM((PIECE, 256), F32),
            pltpu.VMEM((128, 256), BF),
            pltpu.VMEM((1152, 256), BF),
            pltpu.VMEM((4, 256, 256), BF),
            pltpu.VMEM((9, 256, 256), BF),
            pltpu.VMEM((3, 144, 256), BF),
            pltpu.SemaphoreType.DMA((3,)),
        ],
        compiler_params=pltpu.CompilerParams(vmem_limit_bytes=20 << 20),
    )(
        pltpu.with_memory_space_constraint(received, pltpu.VMEM),
        held(heads),
        w_proj[1024:],
        biases,
        b_branch[4:5],
        b_proj[None],
        blend,
        low_taps,
        held(w_dec_up),
        held(w_dec_low.reshape(3, 144, 256)),
        b_dec[None],
    )
    return (context, decoded)


def solution(mesh):
    names = [name for name, size in SPLIT]
    sizes = [size for name, size in SPLIT]
    fine_mesh = Mesh(mesh.devices.reshape(sizes), names)
    in_specs = (
        P(ROWS, None, CHAN),
        P(ROWS, CHAN, None),
        P(CHAN, None),
        P(None, None, CHAN, ROWS),
        P(CHAN, None),
        P(),
        P(),
        P(),
        P(),
        P(),
        P(),
        P(),
        P(),
    )
    out_specs = (P(ROWS, CHAN, None), P(ROWS, CHAN, None))

    return jax.shard_map(
        on_device, mesh=fine_mesh, in_specs=in_specs, out_specs=out_specs, check_vma=False
    )
```
